32 devices in a mesh: seq: 8 (over y, x, core), head: 4 (over z).
Axes of the slice: x: 2, y: 2, z: 4, core: 2. Of those that a mesh axis runs over, the one named last changes fastest.
Arguments:
- tokens: bfloat16 [2, 2, 4096, 1536], P(None, None, 'seq'), may hold values from -6 to 6
- norm_gain: float32 [1536], replicated, may hold values from 0.1 to 1.9
- w_z: bfloat16 [1536, 3072], P('seq', 'head'), may hold values from -0.15625 to 0.15625
- w_x: bfloat16 [1536, 3072], P('seq', 'head'), may hold values from -0.15625 to 0.15625
- w_bc: bfloat16 [1536, 256], P('seq'), may hold values from -0.15625 to 0.15625
- w_dt: bfloat16 [1536, 48], P('seq', 'head'), may hold values from -0.15625 to 0.15625
- conv_x: float32 [4, 3072], P(None, 'head'), may hold values from -3 to 3
- conv_x_bias: float32 [3072], P('head'), may hold values from -2 to 2
- conv_bc: float32 [4, 256], replicated, may hold values from -3 to 3
- conv_bc_bias: float32 [256], replicated, may hold values from -2 to 2
- dt_bias: float32 [48], P('head'), may hold values from -6 to -2
- a_log: float32 [48], P('head'), may hold values from -3 to 1
- d_skip: float32 [48], P('head'), may hold values from 0.5 to 1.5
- gate_gain: float32 [3072], P('head'), may hold values from 0.1 to 1.9
- w_out: bfloat16 [3072, 1536], P('head', 'seq'), may hold values from -0.109375 to 0.109375
- lengths: int32 [2, 2], replicated, may hold values from 1024 to 4096, as said below
- out_grad: bfloat16 [2, 2, 4096, 1536], P(None, None, 'seq'), may hold values from -6 to 6
Outputs:
- layer_out: bfloat16 [2, 2, 4096, 1536], P(None, None, 'seq')
- tokens_grad: bfloat16 [2, 2, 4096, 1536], P(None, None, 'seq')
- norm_gain_grad: float32 [1536], replicated
- w_z_grad: float32 [1536, 3072], P('seq', 'head')
- w_x_grad: float32 [1536, 3072], P('seq', 'head')
- w_bc_grad: float32 [1536, 256], P('seq')
- w_dt_grad: float32 [1536, 48], P('seq', 'head')
- conv_x_grad: float32 [4, 3072], P(None, 'head')
- conv_x_bias_grad: float32 [3072], P('head')
- conv_bc_grad: float32 [4, 256], replicated
- conv_bc_bias_grad: float32 [256], replicated
- dt_bias_grad: float32 [48], P('head')
- a_log_grad: float32 [48], P('head')
- d_skip_grad: float32 [48], P('head')
- gate_gain_grad: float32 [3072], P('head')
- w_out_grad: float32 [3072, 1536], P('head', 'seq')
The draws below stay inside these ranges and needn't reach their ends.
Inputs may be any that keep to these rules, and one draw needn't show every extreme that they name: `lengths`: the first sequence of the first micro-batch uses all 4096 slots.
All inputs are finite; a program needn't handle non-finite values.
Results may differ from the reference program's by a relative error of at most 0.028.
Values may be sent and summed in bfloat16 or wider, within the bound.
A program may use at most 256 MiB of HBM per device.

```python
import math
import jax
import jax.numpy as jnp
from jax import lax

D = 1536
HEADS = 48
HEAD_DIM = 64
NST = 128
CONV = 4
MICRO = 2
SEQS = 2
DI = 3072
LEN = 4096


def draw_lengths(key, part):
    values = jax.random.randint(key, (MICRO, SEQS), LEN // 4, LEN + 1, dtype=jnp.int32)
    return values.at[0, 0].set(LEN)


def block_scale(key, shape, cuts, least, top_value):
    level, own = 1.0, jax.random.fold_in(key, 6)
    for position, blocks in cuts:
        steps = jnp.exp(jax.random.uniform(jax.random.fold_in(own, position), (blocks,), jnp.float32, least / len(cuts), top_value / len(cuts)))
        level = level * jnp.repeat(steps, shape[position] // blocks).reshape([-1 if axis == position else 1 for axis in range(len(shape))])
    return level


def noise(stream_key, dims, spread, limit, cuts=(), kind=jnp.bfloat16):
    array = jax.random.normal(stream_key, dims, jnp.float32) * spread
    if len(cuts) > 0:
        array = block_scale(stream_key, dims, cuts, -0.22, 0.18) * array
    return jnp.clip(array, min=-limit, max=limit).astype(kind)


def setup_inputs(seed: int = 0) -> dict:
    keys = jax.random.split(jax.random.key(seed), 18)
    tokens = noise(keys[0], (MICRO, SEQS, LEN, D), 1.0, 6.0, ((2, 8),))
    norm_gain = jnp.clip(1.0 + 0.18 * jax.random.normal(keys[1], (D,), jnp.float32), 0.1, 1.9)
    w_z = noise(keys[2], (D, DI), D ** -0.5, 0.15625, ((0, 8), (1, 4)))
    w_x = noise(keys[3], (D, DI), D ** -0.5, 0.15625, ((0, 8), (1, 4)))
    w_bc = noise(keys[4], (D, 2 * NST), D ** -0.5, 0.15625, ((0, 8),))
    w_dt = noise(keys[5], (D, HEADS), D ** -0.5, 0.15625, ((0, 8), (1, 4)))
    conv_x = noise(keys[6], (CONV, DI), CONV ** -0.5, 3.0, ((1, 4),), jnp.float32)
    conv_x_bias = noise(keys[7], (DI,), 0.5, 2.0, ((0, 4),), jnp.float32)
    conv_bc = noise(keys[8], (CONV, 2 * NST), CONV ** -0.5, 3.0, (), jnp.float32)
    conv_bc_bias = noise(keys[9], (2 * NST,), 0.5, 2.0, (), jnp.float32)
    dt_bias = jnp.clip(-6.0 + 4.0 * jax.random.uniform(keys[10], (HEADS,), jnp.float32) ** block_scale(keys[10], (HEADS,), ((0, 4),), -0.2, 0.2), -6.0, -2.0)
    a_log = jnp.clip(-3.0 + 4.0 * jax.random.uniform(keys[11], (HEADS,), jnp.float32) ** block_scale(keys[11], (HEADS,), ((0, 4),), -0.2, 0.2), -3.0, 1.0)
    d_skip = jnp.clip(0.5 + 1.0 * jax.random.uniform(keys[12], (HEADS,), jnp.float32) ** block_scale(keys[12], (HEADS,), ((0, 4),), -0.2, 0.2), 0.5, 1.5)
    gate_gain = jnp.clip(1.0 + 0.18 * jax.random.normal(keys[13], (DI,), jnp.float32), 0.1, 1.9)
    w_out = noise(keys[14], (DI, D), DI ** -0.5, 0.109375, ((0, 4), (1, 8)))
    lengths = draw_lengths(jax.random.fold_in(keys[17], 71), 0)
    out_grad = noise(keys[16], (MICRO, SEQS, LEN, D), 1.0, 6.0, ((2, 8),))
    return dict(tokens=tokens, norm_gain=norm_gain, w_z=w_z, w_x=w_x, w_bc=w_bc, w_dt=w_dt, conv_x=conv_x, conv_x_bias=conv_x_bias, conv_bc=conv_bc, conv_bc_bias=conv_bc_bias, dt_bias=dt_bias, a_log=a_log, d_skip=d_skip, gate_gain=gate_gain, w_out=w_out, lengths=lengths, out_grad=out_grad)


epsilon = 1e-05
PRECISE = lax.Precision.HIGHEST

@jax.custom_vjp
def low(v):
    return lax.optimization_barrier(v.astype(jnp.bfloat16)).astype(jnp.float32)

@jax.custom_vjp
def low_back(v):
    return v

def low_keep(v):
    return (low(v), None)

def low_pass(kept, grad):
    return (grad,)

def back_keep(v):
    return (v, None)

def back_low(kept, grad):
    return (low(grad),)
low.defvjp(low_keep, low_pass)
low_back.defvjp(back_keep, back_low)

def ssd_scan(inner_x, b_in, c_in, log_decay, step_size):
    length = inner_x.shape[0]
    block_len = math.gcd(length, 256)
    block_count = length // block_len
    head_count = inner_x.shape[1]

    def one_block(state_now, pieces):
        inner_blk, b_blk, c_blk, decay_blk, step_blk = pieces
        cumul = jnp.cumsum(decay_blk, axis=0)
        positions = jnp.arange(block_len)
        causal = (positions[:, None] >= positions[None, :])[:, :, None]
        differ = cumul[:, None, :] - cumul[None, :, :]
        weights = jnp.where(causal, jnp.exp(jnp.where(causal, differ, 0.0)), 0.0)
        scores = jnp.einsum('tn,sn->ts', c_blk, b_blk, precision=PRECISE)
        mixing = weights * scores[:, :, None]
        scaled = inner_blk * step_blk[:, :, None]
        local_part = jnp.einsum('tsh,shp->thp', mixing, scaled, precision=PRECISE)
        carried = jnp.exp(cumul)[:, :, None] * jnp.einsum('hpn,tn->thp', state_now, c_blk, precision=PRECISE)
        tail_decay = jnp.exp(cumul[-1][None, :] - cumul)
        fresh = jnp.einsum('shp,sn->hpn', (tail_decay * step_blk)[:, :, None] * inner_blk, b_blk, precision=PRECISE)
        state_next = jnp.exp(cumul[-1])[:, None, None] * state_now + fresh
        return (state_next, local_part + carried)
    pieces = (inner_x.reshape(block_count, block_len, head_count, HEAD_DIM), b_in.reshape(block_count, block_len, NST), c_in.reshape(block_count, block_len, NST), log_decay.reshape(block_count, block_len, head_count), step_size.reshape(block_count, block_len, head_count))
    start_state = jnp.zeros((head_count, HEAD_DIM, NST), jnp.float32)
    _, outputs = lax.scan(jax.checkpoint(one_block), start_state, pieces)
    return outputs.reshape(length, head_count, HEAD_DIM)

def layer(hidden, valid_mask, weight_set):
    norm_gain, w_z, w_x, w_bc, w_dt, conv_x, conv_x_bias, conv_bc, conv_bc_bias, dt_bias, a_log, d_skip, gate_gain, w_out = weight_set
    length = hidden.shape[0]
    inverse_rms = lax.rsqrt(lax.optimization_barrier(jnp.mean(hidden * hidden, axis=-1, keepdims=True)) + epsilon)
    normed = low(hidden * inverse_rms * norm_gain)
    gate_z = low_back(jnp.dot(normed, w_z, precision=PRECISE))
    inner_pre = low(low_back(jnp.dot(normed, w_x, precision=PRECISE)))
    bc_pre = low(low_back(jnp.dot(normed, w_bc, precision=PRECISE)))
    dt_raw = low_back(jnp.dot(normed, w_dt, precision=PRECISE))
    joined = jnp.concatenate([inner_pre, bc_pre], axis=1)
    kernel = jnp.concatenate([conv_x, conv_bc], axis=1)
    conv_bias = jnp.concatenate([conv_x_bias, conv_bc_bias])
    padded = jnp.concatenate([jnp.zeros((CONV - 1, joined.shape[1]), jnp.float32), joined], axis=0)
    conv_out = conv_bias + kernel[0] * padded[0:length]
    for offset in range(1, CONV):
        conv_out = conv_out + kernel[offset] * padded[offset:offset + length]
    acted = jax.nn.silu(conv_out)
    inner_x = acted[:, :DI].reshape(length, HEADS, HEAD_DIM)
    b_in = acted[:, DI:DI + NST]
    c_in = acted[:, DI + NST:]
    step_size = jax.nn.softplus(dt_raw + dt_bias)
    log_decay = -jnp.exp(a_log) * step_size
    ssd_out = ssd_scan(inner_x, b_in, c_in, log_decay, step_size) + d_skip[:, None] * inner_x
    gated_out = ssd_out.reshape(length, DI) * jax.nn.silu(gate_z)
    inverse_gate = lax.rsqrt(lax.optimization_barrier(jnp.mean(gated_out * gated_out, axis=-1, keepdims=True)) + epsilon)
    gate_normed = low(gated_out * inverse_gate * gate_gain)
    branch = low_back(jnp.dot(gate_normed, w_out, precision=PRECISE))
    return hidden + valid_mask[:, None] * branch

def reference(tokens, norm_gain, w_z, w_x, w_bc, w_dt, conv_x, conv_x_bias, conv_bc, conv_bc_bias, dt_bias, a_log, d_skip, gate_gain, w_out, lengths, out_grad):
    weight_set = (norm_gain.astype(jnp.float32), w_z.astype(jnp.float32), w_x.astype(jnp.float32), w_bc.astype(jnp.float32), w_dt.astype(jnp.float32), conv_x.astype(jnp.float32), conv_x_bias.astype(jnp.float32), conv_bc.astype(jnp.float32), conv_bc_bias.astype(jnp.float32), dt_bias.astype(jnp.float32), a_log.astype(jnp.float32), d_skip.astype(jnp.float32), gate_gain.astype(jnp.float32), w_out.astype(jnp.float32))
    hidden_all = tokens.astype(jnp.float32).reshape(MICRO * SEQS, LEN, D)
    positions = jnp.arange(LEN, dtype=jnp.int32)
    valid_all = (positions[None, :] < lengths.reshape(MICRO * SEQS)[:, None].astype(jnp.int32)).astype(jnp.float32)
    checked_layer = jax.checkpoint(layer)

    def forward(weights_in, hidden_in):

        def per_sequence(carry_value, pieces):
            return (carry_value, checked_layer(pieces[0], pieces[1], weights_in))
        _, outputs = lax.scan(per_sequence, jnp.zeros((), jnp.float32), (hidden_in, valid_all))
        return outputs
    outputs, pullback = jax.vjp(forward, weight_set, hidden_all)
    weight_grads, hidden_grads = pullback(out_grad.astype(jnp.float32).reshape(MICRO * SEQS, LEN, D))
    return (outputs.reshape(MICRO, SEQS, LEN, D).astype(jnp.bfloat16), hidden_grads.reshape(MICRO, SEQS, LEN, D).astype(jnp.bfloat16), weight_grads[0], weight_grads[1], weight_grads[2], weight_grads[3], weight_grads[4], weight_grads[5], weight_grads[6], weight_grads[7], weight_grads[8], weight_grads[9], weight_grads[10], weight_grads[11], weight_grads[12], weight_grads[13])
```

```python
import functools

import jax
import jax.numpy as jnp
from jax import lax
from jax.experimental import pallas as pl
from jax.experimental.pallas import tpu as pltpu
from jax.sharding import PartitionSpec as P

HEAD_DIM = 64
NST = 128
CONV = 4
CHUNK = 128
LANES = 128
EDGE = 8
GROUPS = 4

epsilon = 1e-05
f32 = jnp.float32
bf16 = jnp.bfloat16

NN = (((1,), (0,)), ((), ()))
NT = (((1,), (1,)), ((), ()))
TN = (((0,), (0,)), ((), ()))


def mm(a, b, dims=NN):
    return lax.dot_general(a, b, dims, preferred_element_type=f32)


def mm_split(a, b, dims=NN):
    high = a.astype(bf16)
    low = (a - high.astype(f32)).astype(bf16)
    return mm(high, b, dims) + mm(low, b, dims)


def mm_split_right(a, b, dims=NN):
    high = b.astype(bf16)
    rest = b - high.astype(f32)
    mid = rest.astype(bf16)
    low = (rest - mid.astype(f32)).astype(bf16)
    return mm(a, high, dims) + (mm(a, mid, dims) + mm(a, low, dims))


def sigmoid(v):
    return 1.0 / (1.0 + jnp.exp(-v))


def softplus(v):
    return jnp.maximum(v, 0.0) + jnp.log1p(jnp.exp(-jnp.abs(v)))


def iotas(rows, cols):
    return (
        lax.broadcasted_iota(jnp.int32, (rows, cols), 0),
        lax.broadcasted_iota(jnp.int32, (rows, cols), 1),
    )


def lower_ones():
    row, col = iotas(CHUNK, CHUNK)
    return (row >= col).astype(bf16)


def conv_rows(ext, taps, rows):
    total = taps[CONV : CONV + 1, :] + taps[0:1, :] * ext[EDGE - 3 : EDGE - 3 + rows, :]
    for k in range(1, CONV):
        total = total + taps[k : k + 1, :] * ext[EDGE - 3 + k : EDGE - 3 + k + rows, :]
    return total


def chunk_decays(dt_raw, heads_ref):
    step = softplus(dt_raw + heads_ref[0:1, :])
    log_decay = -jnp.exp(heads_ref[1:2, :]) * step
    cumul = mm_split_right(lower_ones(), log_decay)
    return step, cumul


def pair_weights(cumul, cumul_t, head, causal):
    differ = cumul[:, head : head + 1] - cumul_t[head : head + 1, :]
    return jnp.exp(jnp.where(causal, differ, -1e30))


def block_diag(pair, low_lanes):
    zero = jnp.zeros_like(pair)
    return jnp.concatenate(
        [jnp.where(low_lanes, pair, zero), jnp.where(low_lanes, zero, pair)], axis=0
    )


def project_kernel(
    tok_ref,
    halo_ref,
    gain_ref,
    w_ref,
    taps_ref,
    heads_ref,
    spread_ref,
    normed_ref,
    proj_ref,
    dt_ref,
    acted_ref,
    local_ref,
    cumul_ref,
    states_ref,
    total_ref,
    edge_ref,
    joined,
    state,
):
    rows = tok_ref.shape[1]
    width = spread_ref.shape[1]
    wide = width + 2 * NST
    tile = 384

    def norm(v):
        v = v.astype(f32)
        inverse = lax.rsqrt(jnp.mean(v * v, axis=-1, keepdims=True) + epsilon)
        return (v * inverse * gain_ref[...]).astype(bf16)

    edge = mm(norm(halo_ref[0]), w_ref[:, width : 2 * width + 2 * NST])
    edge = edge.astype(bf16).astype(f32)[EDGE:, :]
    joined[0:EDGE, :] = edge
    edge_ref[0] = edge
    normed_ref[0] = norm(tok_ref[0])
    for start in range(0, 2 * width, tile):
        part = mm(normed_ref[0], w_ref[:, start : start + tile]).astype(bf16)
        proj_ref[0, :, start : start + tile] = part
        if start >= width:
            joined[EDGE:, start - width : start - width + tile] = part.astype(f32)
    last = mm(normed_ref[0], w_ref[:, 2 * width :])
    part = last[:, : 2 * NST].astype(bf16)
    proj_ref[0, :, 2 * width :] = part
    joined[EDGE:, width:] = part.astype(f32)
    dt_ref[0] = last[:, 2 * NST :]

    row, col = iotas(CHUNK, CHUNK)
    causal = row >= col
    low_lanes = col < HEAD_DIM
    state[...] = jnp.zeros_like(state)

    def chunk(index, base):
        start = pl.multiple_of(index * CHUNK, CHUNK)
        here = pl.ds(start, CHUNK)
        conv = conv_rows(joined[pl.ds(start, CHUNK + EDGE), :], taps_ref, CHUNK)
        acted = conv * sigmoid(conv)
        acted_low = acted.astype(bf16)
        acted_ref[0, here, :] = acted_low
        b_low = acted_low[:, width : width + NST]
        c_low = acted_low[:, width + NST :]
        step, cumul = chunk_decays(dt_ref[0, here, :], heads_ref)
        cumul_t = cumul.T
        final = cumul[CHUNK - 1 :, :]
        cumul_ref[0, here, :] = cumul + base
        scaled = mm_split(step, spread_ref[...]) * acted[:, :width]
        scaled_low = scaled.astype(bf16)
        scores = mm(c_low, b_low, NT)
        states_ref[0, pl.ds(index, 1)] = state[...].astype(bf16)[None]
        carried = mm_split(jnp.exp(cumul), spread_ref[...]) * mm(c_low, state[...].astype(bf16))
        for pair in range(width // LANES):
            lanes = slice(pair * LANES, (pair + 1) * LANES)
            mixing = [
                (pair_weights(cumul, cumul_t, 2 * pair + k, causal) * scores).astype(bf16)
                for k in (0, 1)
            ]
            here_out = mm(
                jnp.concatenate(mixing, axis=1), block_diag(scaled_low[:, lanes], low_lanes)
            )
            local_ref[0, here, lanes] = (here_out + carried[:, lanes]).astype(bf16)
        tail = mm_split(jnp.exp(final - cumul), spread_ref[...])
        fresh = mm(b_low, (scaled * tail).astype(bf16), TN)
        keep = mm_split(jnp.broadcast_to(jnp.exp(final), (EDGE, LANES)), spread_ref[...])[0:1, :]
        state[...] = keep * state[...] + fresh
        return base + final

    base = lax.fori_loop(0, rows // CHUNK, chunk, jnp.zeros((1, LANES), f32))
    total_ref[0, 0:NST, :] = state[...].astype(bf16)
    decay = mm_split(jnp.broadcast_to(jnp.exp(base), (2 * EDGE, LANES)), spread_ref[...])
    high = decay.astype(bf16)
    first = lax.broadcasted_iota(jnp.int32, decay.shape, 0) == 0
    total_ref[0, NST:, :] = jnp.where(first, high.astype(f32), decay - high.astype(f32)).astype(bf16)


def gate_kernel(
    acted_ref,
    local_ref,
    cumul_ref,
    z_ref,
    enter_ref,
    grad_ref,
    w_out_ref,
    spread_ref,
    chan_ref,
    ssd_ref,
    gn_ref,
    sums_ref,
):
    rows = acted_ref.shape[1]
    width = spread_ref.shape[1]
    gn_ref[0] = mm(grad_ref[0], w_out_ref[...], NT).astype(bf16)

    def chunk(index, carry):
        here = pl.ds(pl.multiple_of(index * CHUNK, CHUNK), CHUNK)
        c_low = acted_ref[0, here, width + NST :]
        carried = mm_split(jnp.exp(cumul_ref[0, here, :]), spread_ref[...]) * mm(
            c_low, enter_ref[0]
        )
        ssd = (
            local_ref[0, here, :].astype(f32)
            + carried
            + chan_ref[1:2, :] * acted_ref[0, here, :width].astype(f32)
        )
        ssd_low = ssd.astype(bf16)
        ssd_ref[0, here, :] = ssd_low
        gate = z_ref[0, here, :].astype(f32)
        gated = ssd_low.astype(f32) * (gate * sigmoid(gate))
        square = jnp.sum(gated * gated, axis=-1, keepdims=True)
        inner = jnp.sum(
            gn_ref[0, here, :].astype(f32) * chan_ref[0:1, :] * gated, axis=-1, keepdims=True
        )
        _, col = iotas(CHUNK, LANES)
        both = jnp.where(col == 0, square, jnp.where(col == 1, inner, 0.0))
        sums_ref[0, :, here] = both.T[0:EDGE, :]
        return carry

    lax.fori_loop(0, rows // CHUNK, chunk, 0)


def mixer_kernel(
    sums_ref,
    ssd_ref,
    z_ref,
    gn_ref,
    acted_ref,
    dt_ref,
    cumul_ref,
    states_ref,
    enter_ref,
    w_out_ref,
    heads_ref,
    spread_ref,
    chan_ref,
    gnorm_ref,
    branch_ref,
    gz_ref,
    dx_ref,
    dbc_ref,
    ddt_ref,
    dld_ref,
    total_ref,
    cols_ref,
    grad_state,
    *,
    inner_total,
):
    rows = acted_ref.shape[1]
    width = spread_ref.shape[1]
    chunks = rows // CHUNK
    row, col = iotas(CHUNK, CHUNK)
    causal = row >= col
    low_lanes = col < HEAD_DIM
    grad_state[...] = jnp.zeros_like(grad_state)
    cols_ref[0] = jnp.zeros_like(cols_ref[0])
    spread = spread_ref[...]

    def chunk(turn, carry):
        index = chunks - 1 - turn
        start = pl.multiple_of(index * CHUNK, CHUNK)
        here = pl.ds(start, CHUNK)
        sums = jnp.concatenate(
            [sums_ref[0, :, here], jnp.zeros((CHUNK - EDGE, CHUNK), f32)], axis=0
        ).T
        inverse = lax.rsqrt(sums[:, 0:1] / inner_total + epsilon)
        inner_mean = inverse * sums[:, 1:2] / inner_total
        gate = z_ref[0, here, :].astype(f32)
        sig = sigmoid(gate)
        silu = gate * sig
        ssd = ssd_ref[0, here, :].astype(f32)
        unit = ssd * silu * inverse
        gnorm_ref[0, here, :] = (unit * chan_ref[0:1, :]).astype(bf16)
        gn = gn_ref[0, here, :].astype(f32)
        grad_gated = inverse * (gn * chan_ref[0:1, :] - unit * inner_mean)
        grad_ssd = grad_gated * silu
        gz_ref[0, here, :] = (grad_gated * ssd * sig * (1.0 + gate * (1.0 - sig))).astype(bf16)
        x_low = acted_ref[0, here, :width]
        x = x_low.astype(f32)
        b_low = acted_ref[0, here, width : width + NST]
        c_low = acted_ref[0, here, width + NST :]
        cols_ref[0, 0:1, :] += jnp.sum(gn * unit, axis=0, keepdims=True)
        cols_ref[0, 1:2, :] += jnp.sum(x * grad_ssd, axis=0, keepdims=True)

        step, cumul = chunk_decays(dt_ref[0, here, :], heads_ref)
        cumul_t = cumul.T
        final = cumul[CHUNK - 1 :, :]
        before = cumul_ref[0, here, :][0:1, :] - cumul[0:1, :]
        step_wide = mm_split(step, spread)
        scaled = step_wide * x
        scaled_low = scaled.astype(bf16)
        dy_low = grad_ssd.astype(bf16)
        dy = dy_low.astype(f32)
        grown = mm_split(jnp.exp(cumul), spread)
        tail = mm_split(jnp.exp(final - cumul), spread)
        keeps = mm_split(
            jnp.concatenate(
                [
                    jnp.broadcast_to(jnp.exp(final), (EDGE, LANES)),
                    jnp.broadcast_to(jnp.exp(before), (EDGE, LANES)),
                ],
                axis=0,
            ),
            spread,
        )
        keep = keeps[0:1, :]
        state = (
            states_ref[0, pl.ds(index, 1)][0].astype(f32)
            + keeps[EDGE : EDGE + 1, :] * enter_ref[0].astype(f32)
        )
        state_low = state.astype(bf16)
        later = grad_state[...]
        later_low = later.astype(bf16)
        scores = mm(c_low, b_low, NT)
        carried = grown * mm(c_low, state_low)
        tail_grad = tail * mm(b_low, later_low)
        score_grad = jnp.zeros((CHUNK, CHUNK), f32)
        rising = []
        falling = []
        for pair in range(width // LANES):
            lanes = slice(pair * LANES, (pair + 1) * LANES)
            decays = [pair_weights(cumul, cumul_t, 2 * pair + k, causal) for k in (0, 1)]
            mixing = [(d * scores).astype(bf16) for d in decays]
            scaled_two = block_diag(scaled_low[:, lanes], low_lanes)
            dy_two = block_diag(dy_low[:, lanes], low_lanes)
            out = mm(jnp.concatenate(mixing, axis=1), scaled_two)
            mixing_grad = mm(dy_low[:, lanes], scaled_two, NT)
            own_grad = mm(jnp.concatenate(mixing, axis=0), dy_two, TN)
            score_grad = (
                score_grad
                + mixing_grad[:, :CHUNK] * decays[0]
                + mixing_grad[:, CHUNK:] * decays[1]
            )
            scaled_back = scaled_low[:, lanes].astype(f32)
            rising.append(
                dy[:, lanes] * (out + carried[:, lanes]) - scaled_back * own_grad
            )
            falling.append(own_grad)
        own_all = jnp.concatenate(falling, axis=1)
        scaled_grad = own_all + tail_grad
        rise = mm_split(jnp.concatenate(rising, axis=1), spread, NT)
        fall = mm_split(scaled * tail_grad, spread, NT)
        dx_ref[0, here, :] = (step_wide * scaled_grad + chan_ref[1:2, :] * grad_ssd).astype(bf16)
        ddt_ref[0, here, :] = mm_split(x * scaled_grad, spread, NT)
        at_end = mm_split(
            jnp.broadcast_to(jnp.sum(later * state * keep, axis=0, keepdims=True), (EDGE, width)),
            spread,
            NT,
        )[0:1, :]
        upper = (row <= col).astype(bf16)
        under = (row > col).astype(bf16)
        dld_ref[0, here, :] = mm_split_right(upper, rise) + mm_split_right(under, fall) + at_end
        score_low = score_grad.astype(bf16)
        dy_grown = (dy * grown).astype(bf16)
        db = mm(score_low, c_low, TN) + mm((scaled * tail).astype(bf16), later_low, NT)
        dc = mm(score_low, b_low) + mm(dy_grown, state_low, NT)
        dbc_ref[0, here, 0:NST] = db
        dbc_ref[0, here, NST:] = dc
        grad_state[...] = keep * later + mm(c_low, dy_grown, TN)
        return carry

    lax.fori_loop(0, chunks, chunk, 0)
    total_ref[0] = grad_state[...].astype(bf16)
    branch_ref[0] = mm(gnorm_ref[0], w_out_ref[...]).astype(bf16)


def conv_kernel(
    proj_ref,
    edge_ref,
    acted_ref,
    dx_ref,
    dbc_ref,
    ddt_ref,
    dld_ref,
    dt_ref,
    cumul_ref,
    enter_ref,
    leave_ref,
    taps_ref,
    heads_ref,
    spread_ref,
    gj_ref,
    gdt_ref,
    first_ref,
    tapsum_ref,
    headsum_ref,
    joined,
    grads,
):
    rows = acted_ref.shape[1]
    width = spread_ref.shape[1]
    chunks = rows // CHUNK
    spread = spread_ref[...]
    joined[0:EDGE, :] = edge_ref[0]
    joined[EDGE:, :] = proj_ref[0, :, width:].astype(f32)
    tapsum_ref[0] = jnp.zeros_like(tapsum_ref[0])
    headsum_ref[0] = jnp.zeros_like(headsum_ref[0])
    grads[rows:, :] = jnp.zeros((EDGE, width + 2 * NST), f32)
    leave = leave_ref[0]
    enter = enter_ref[0]
    final = cumul_ref[0, rows - EDGE :, :][EDGE - 1 :, :]
    held = jnp.sum(leave.astype(f32) * enter.astype(f32), axis=0, keepdims=True)
    at_end = mm_split(jnp.broadcast_to(held, (EDGE, width)), spread, NT)[0:1, :] * jnp.exp(final)
    row, col = iotas(CHUNK, CHUNK)
    under = (row > col).astype(bf16)
    rate = jnp.exp(heads_ref[1:2, :])

    def chunk(index, passed):
        start = pl.multiple_of(index * CHUNK, CHUNK)
        here = pl.ds(start, CHUNK)
        conv_ext = joined[pl.ds(start, CHUNK + EDGE), :]
        conv = conv_rows(conv_ext, taps_ref, CHUNK)
        sig = sigmoid(conv)
        slope = sig * (1.0 + conv * (1.0 - sig))
        x = acted_ref[0, here, :width].astype(f32)
        b_low = acted_ref[0, here, width : width + NST]
        raw = dt_ref[0, here, :] + heads_ref[0:1, :]
        step = softplus(raw)
        step_wide = mm_split(step, spread)
        tail = mm_split(jnp.exp(final - cumul_ref[0, here, :]), spread)
        tail_grad = tail * mm(b_low, leave)
        scaled = step_wide * x
        dx = dx_ref[0, here, :].astype(f32) + step_wide * tail_grad
        db = dbc_ref[0, here, 0:NST] + mm((scaled * tail).astype(bf16), leave, NT)
        dc = dbc_ref[0, here, NST:]
        moved = mm_split(x * tail_grad, spread, NT)
        fall = moved * step
        dstep = ddt_ref[0, here, :] + moved
        dld = dld_ref[0, here, :] + mm_split_right(under, fall) + passed + at_end
        gdt = (dstep - rate * dld) * sigmoid(raw)
        gdt_ref[0, here, :] = gdt.astype(bf16)
        headsum_ref[0, 0:1, :] += jnp.sum(gdt, axis=0, keepdims=True)
        headsum_ref[0, 1:2, :] += -rate * jnp.sum(step * dld, axis=0, keepdims=True)
        grad = jnp.concatenate([dx, db, dc], axis=1) * slope
        grads[here, :] = grad
        for k in range(CONV):
            tapsum_ref[0, k : k + 1, :] += jnp.sum(
                grad * conv_ext[EDGE - 3 + k : EDGE - 3 + k + CHUNK, :], axis=0, keepdims=True
            )
        tapsum_ref[0, CONV : CONV + 1, :] += jnp.sum(grad, axis=0, keepdims=True)
        return passed + jnp.sum(fall, axis=0, keepdims=True)

    lax.fori_loop(0, chunks, chunk, jnp.zeros((1, LANES), f32))
    first_ref[0] = grads[0:EDGE, :]

    def back(index, carry):
        start = pl.multiple_of(index * CHUNK, CHUNK)
        ext = grads[pl.ds(start, CHUNK + EDGE), :]
        total = taps_ref[CONV - 1 : CONV, :] * ext[0:CHUNK, :]
        for k in range(CONV - 1):
            total = total + taps_ref[k : k + 1, :] * ext[3 - k : 3 - k + CHUNK, :]
        gj_ref[0, pl.ds(start, CHUNK), :] = total.astype(bf16)
        return carry

    lax.fori_loop(0, chunks, back, 0)


def input_kernel(gz_ref, gj_ref, gdt_ref, next_ref, taps_ref, w_ref, fixed_ref, out_ref):
    rows = gz_ref.shape[1]
    width = gz_ref.shape[2]
    wide = gj_ref.shape[2]
    ext = jnp.concatenate([jnp.zeros((2 * EDGE, wide), f32), next_ref[0]], axis=0)
    extra = jnp.zeros((2 * EDGE, wide), f32)
    for k in range(CONV - 1):
        extra = extra + taps_ref[k : k + 1, :] * ext[3 - k : 3 - k + 2 * EDGE, :]
    fixed_ref[0] = gj_ref[0]
    tail = slice(rows - 2 * EDGE, rows)
    fixed_ref[0, tail, :] = (gj_ref[0, tail, :].astype(f32) + extra).astype(bf16)
    tile = 384
    for start in range(0, out_ref.shape[2], tile):
        part = slice(start, start + tile)
        total = mm(gz_ref[0], w_ref[part, :width], NT)
        total = total + mm(fixed_ref[0], w_ref[part, width : width + wide], NT)
        total = total + mm(gdt_ref[0], w_ref[part, width + wide :], NT)
        out_ref[0, :, part] = total.astype(bf16)


def per_sequence(shape):
    zeros = (0,) * (len(shape) - 1)
    return pl.BlockSpec((1,) + tuple(shape[1:]), lambda i: (i,) + zeros)


def whole(shape):
    zeros = (0,) * len(shape)
    return pl.BlockSpec(tuple(shape), lambda i: zeros, pipeline_mode=pl.Buffered(1))


def run(body, name, count, streamed, fixed, outs, scratch, flops, order=None):
    operands = list(streamed) + list(fixed)
    moved = sum(a.size * a.dtype.itemsize for a in operands)
    moved += sum(o.size * o.dtype.itemsize for o in outs)
    return pl.pallas_call(
        body,
        name=name,
        grid=(count,),
        in_specs=[per_sequence(a.shape) for a in streamed] + [whole(a.shape) for a in fixed],
        out_specs=[per_sequence(o.shape) for o in outs],
        out_shape=outs,
        scratch_shapes=scratch,
        compiler_params=pltpu.CompilerParams(vmem_limit_bytes=60 * 1024 * 1024),
        cost_estimate=pl.CostEstimate(flops=flops, bytes_accessed=moved, transcendentals=0),
    )(*operands)


def spec(*shape, dtype=f32):
    return jax.ShapeDtypeStruct(shape, dtype)


def exchange(total, axis, forward):
    size = lax.axis_size(axis)
    place = lax.axis_index(axis)
    state = total[:, :NST].astype(f32)
    decay = jnp.sum(total[:, NST : NST + 2].astype(f32), axis=1, keepdims=True)
    met = jnp.zeros_like(state)
    met_decay = jnp.ones_like(decay)
    payload = total
    bit = 1
    while bit < size:
        got = lax.ppermute(payload, axis, [(i, i ^ bit) for i in range(size)])
        other = got[:, :NST].astype(f32)
        other_decay = jnp.sum(got[:, NST : NST + 2].astype(f32), axis=1, keepdims=True)
        upper = (place & bit) != 0
        earlier = upper if forward else jnp.logical_not(upper)
        met = jnp.where(earlier, met_decay * other + met, met)
        met_decay = jnp.where(earlier, met_decay * other_decay, met_decay)
        bit *= 2
        if bit < size:
            state = jnp.where(earlier, decay * other + state, other_decay * state + other)
            decay = decay * other_decay
            high = decay.astype(bf16)
            low = (decay - high.astype(f32)).astype(bf16)
            payload = jnp.concatenate(
                [state.astype(bf16), high, low, jnp.zeros_like(total[:, NST + 2 :])], axis=1
            )
    return met.astype(bf16)


def local(
    tokens,
    norm_gain,
    w_z,
    w_x,
    w_bc,
    w_dt,
    conv_x,
    conv_x_bias,
    conv_bc,
    conv_bc_bias,
    dt_bias,
    a_log,
    d_skip,
    gate_gain,
    w_out,
    lengths,
    out_grad,
):
    micro, seqs, rows, model = tokens.shape
    batch = micro * seqs
    width = w_z.shape[1]
    heads = width // HEAD_DIM
    wide = width + 2 * NST
    inner_total = width * lax.axis_size("head")
    per = batch // GROUPS
    flat = tokens.reshape(batch, rows, model)
    flat_grad = out_grad.reshape(batch, rows, model)

    seq_size = lax.axis_size("seq")
    halo = lax.ppermute(
        flat[:, rows - 2 * EDGE :, :], "seq", [(i, i + 1) for i in range(seq_size - 1)]
    )
    keep_rows = jnp.arange(2 * EDGE) >= 2 * EDGE - (CONV - 1)
    halo = jnp.where(keep_rows[None, :, None], halo, jnp.zeros_like(halo))

    w_shard = jnp.concatenate(
        [w_z, w_x, w_bc, w_dt, jnp.zeros((w_dt.shape[0], LANES - heads), bf16)], axis=1
    )
    w_all = lax.all_gather(w_shard, "seq", axis=0, tiled=True)
    w_back = lax.all_gather(w_out, "seq", axis=1, tiled=True)

    positions = lax.axis_index("seq") * rows + jnp.arange(rows, dtype=jnp.int32)
    valid = positions[None, :] < lengths.reshape(batch)[:, None]
    grad_branch = jnp.where(valid[:, :, None], flat_grad, jnp.zeros_like(flat_grad))

    taps = jnp.concatenate(
        [
            jnp.concatenate([conv_x, conv_bc], axis=1),
            jnp.concatenate([conv_x_bias, conv_bc_bias])[None],
            jnp.zeros((EDGE - CONV - 1, wide), f32),
        ],
        axis=0,
    )
    pad = LANES - heads
    head_rows = jnp.concatenate(
        [
            jnp.concatenate([dt_bias, jnp.full((pad,), -1e4, f32)])[None],
            jnp.concatenate([a_log, jnp.zeros((pad,), f32)])[None],
            jnp.zeros((EDGE - 2, LANES), f32),
        ],
        axis=0,
    )
    spread = (
        jnp.arange(LANES)[:, None] == (jnp.arange(width) // HEAD_DIM)[None, :]
    ).astype(bf16)
    chan = jnp.concatenate(
        [
            gate_gain[None],
            jnp.repeat(d_skip, HEAD_DIM)[None],
            jnp.zeros((EDGE - 2, width), f32),
        ],
        axis=0,
    )
    chunks = rows // CHUNK

    first = []
    for g in range(GROUPS):
        part = slice(g * per, (g + 1) * per)
        first.append(
            run(
                project_kernel,
                "project",
                per,
                [flat[part], halo[part]],
                [norm_gain[None], w_all, taps, head_rows, spread],
                [
                    spec(per, rows, model, dtype=bf16),
                    spec(per, rows, 2 * width + 2 * NST, dtype=bf16),
                    spec(per, rows, LANES),
                    spec(per, rows, wide, dtype=bf16),
                    spec(per, rows, width, dtype=bf16),
                    spec(per, rows, LANES),
                    spec(per, chunks, NST, width, dtype=bf16),
                    spec(per, NST + 2 * EDGE, width, dtype=bf16),
                    spec(per, EDGE, wide),
                ],
                [pltpu.VMEM((rows + EDGE, wide), f32), pltpu.VMEM((NST, width), f32)],
                2 * per * rows * model * w_all.shape[1],
            )
        )
    entering = [exchange(first[g][7], "seq", True) for g in range(GROUPS)]

    second = []
    for g in range(GROUPS):
        part = slice(g * per, (g + 1) * per)
        _, proj, _, acted, own, cumul, _, _, _ = first[g]
        second.append(
            run(
                gate_kernel,
                "gate",
                per,
                [acted, own, cumul, proj[:, :, :width], entering[g], grad_branch[part]],
                [w_back, spread, chan],
                [
                    spec(per, rows, width, dtype=bf16),
                    spec(per, rows, width, dtype=bf16),
                    spec(per, EDGE, rows),
                ],
                [],
                2 * per * rows * model * width,
            )
        )
    sums = [lax.psum(second[g][2], "head") for g in range(GROUPS)]

    third = []
    for g in range(GROUPS):
        _, proj, dt_raw, acted, _, cumul, states, _, _ = first[g]
        ssd, gn, _ = second[g]
        third.append(
            run(
                functools.partial(mixer_kernel, inner_total=inner_total),
                "mixer",
                per,
                [
                    sums[g],
                    ssd,
                    proj[:, :, :width],
                    gn,
                    acted,
                    dt_raw,
                    cumul,
                    states,
                    entering[g],
                ],
                [w_back, head_rows, spread, chan],
                [
                    spec(per, rows, width, dtype=bf16),
                    spec(per, rows, model, dtype=bf16),
                    spec(per, rows, width, dtype=bf16),
                    spec(per, rows, width, dtype=bf16),
                    spec(per, rows, 2 * NST),
                    spec(per, rows, LANES),
                    spec(per, rows, LANES),
                    spec(per, NST, width, dtype=bf16),
                    spec(per, EDGE, width),
                ],
                [pltpu.VMEM((NST, width), f32)],
                2 * per * rows * model * width,
            )
        )
    branches = [lax.psum(third[g][1], "head") for g in range(GROUPS)]
    leaving = [
        exchange(
            jnp.concatenate([third[g][7], first[g][7][:, NST:]], axis=1), "seq", False
        )
        for g in range(GROUPS)
    ]

    fourth = []
    for g in range(GROUPS):
        _, proj, dt_raw, acted, _, cumul, _, _, edge = first[g]
        _, _, _, dx, dbc, ddt, dld, _, _ = third[g]
        fourth.append(
            run(
                conv_kernel,
                "conv",
                per,
                [proj, edge, acted, dx, dbc, ddt, dld, dt_raw, cumul, entering[g], leaving[g]],
                [taps, head_rows, spread],
                [
                    spec(per, rows, wide, dtype=bf16),
                    spec(per, rows, LANES, dtype=bf16),
                    spec(per, EDGE, wide),
                    spec(per, EDGE, wide),
                    spec(per, EDGE, LANES),
                ],
                [pltpu.VMEM((rows + EDGE, wide), f32), pltpu.VMEM((rows + EDGE, wide), f32)],
                per * rows * wide * 60,
            )
        )
    nexts = [
        lax.ppermute(fourth[g][2], "seq", [(i + 1, i) for i in range(seq_size - 1)])
        for g in range(GROUPS)
    ]

    fifth = []
    for g in range(GROUPS):
        gj, gdt, _, _, _ = fourth[g]
        fifth.append(
            run(
                input_kernel,
                "input_grad",
                per,
                [third[g][2], gj, gdt, nexts[g]],
                [taps, w_all],
                [spec(per, rows, wide, dtype=bf16), spec(per, rows, model, dtype=bf16)],
                [],
                2 * per * rows * model * w_all.shape[1],
            )
        )
    summed = [lax.psum(fifth[g][1], "head") for g in range(GROUPS)]

    def joined(parts):
        return jnp.concatenate(parts, axis=0).reshape(batch * rows, -1)

    normed = joined([f[0] for f in first])
    gz = joined([t[2] for t in third])
    gj = joined([t[0] for t in fifth])
    gdt = joined([t[1] for t in fourth])
    gnorm = joined([t[0] for t in third])
    w_grad = jnp.concatenate(
        [mm(normed, gz, TN), mm(normed, gj, TN), mm(normed, gdt, TN)], axis=1
    ).astype(bf16)
    out_w_grad = mm(gnorm, grad_branch.reshape(batch * rows, model), TN).astype(bf16)
    w_sum = lax.psum_scatter(w_grad, "seq", scatter_dimension=0, tiled=True)
    out_w_sum = lax.psum_scatter(out_w_grad, "seq", scatter_dimension=1, tiled=True)
    bc_sum = lax.psum(w_sum[:, 2 * width : 2 * width + 2 * NST], "head")

    layer_outs = []
    input_grads = []
    gain_grad = jnp.zeros((model,), f32)
    for g in range(GROUPS):
        part = slice(g * per, (g + 1) * per)
        hidden = flat[part].astype(f32)
        layer_outs.append(
            jnp.where(
                valid[part][:, :, None], hidden + branches[g].astype(f32), hidden
            ).astype(bf16)
        )
        inverse = lax.rsqrt(jnp.mean(hidden * hidden, axis=-1, keepdims=True) + epsilon)
        unit = hidden * inverse
        grad_in = summed[g].astype(f32)
        gain_grad = gain_grad + jnp.sum(grad_in * unit, axis=(0, 1))
        scaled = grad_in * norm_gain
        input_grads.append(
            (
                flat_grad[part].astype(f32)
                + inverse * (scaled - unit * jnp.mean(scaled * unit, axis=-1, keepdims=True))
            ).astype(bf16)
        )

    cols = sum(jnp.sum(t[8], axis=0) for t in third)
    tap_sum = sum(jnp.sum(t[3], axis=0) for t in fourth)
    head_sum = sum(jnp.sum(t[4], axis=0) for t in fourth)
    skip = jnp.sum(cols[1].reshape(heads, HEAD_DIM), axis=1)
    gain_grad, cols0, tap_sum, head_sum, skip = lax.psum(
        (gain_grad, cols[0], tap_sum[: CONV + 1], head_sum[:2], skip), "seq"
    )
    bc_taps = lax.psum(tap_sum[:, width:], "head")

    out_shape = (micro, seqs, rows, model)
    return (
        jnp.concatenate(layer_outs, axis=0).reshape(out_shape),
        jnp.concatenate(input_grads, axis=0).reshape(out_shape),
        gain_grad,
        w_sum[:, :width].astype(f32),
        w_sum[:, width : 2 * width].astype(f32),
        bc_sum.astype(f32),
        w_sum[:, 2 * width + 2 * NST : 2 * width + 2 * NST + heads].astype(f32),
        tap_sum[:CONV, :width],
        tap_sum[CONV, :width],
        bc_taps[:CONV],
        bc_taps[CONV],
        head_sum[0, :heads],
        head_sum[1, :heads],
        skip,
        cols0,
        out_w_sum.astype(f32),
    )


def solution(mesh):
    placed = (
        P(None, None, "seq", None),
        P(),
        P("seq", "head"),
        P("seq", "head"),
        P("seq", None),
        P("seq", "head"),
        P(None, "head"),
        P("head"),
        P(),
        P(),
        P("head"),
        P("head"),
        P("head"),
        P("head"),
        P("head", "seq"),
        P(),
        P(None, None, "seq", None),
    )
    return jax.shard_map(
        local,
        mesh=mesh,
        in_specs=placed,
        out_specs=(
            P(None, None, "seq", None),
            P(None, None, "seq", None),
            P(),
            P("seq", "head"),
            P("seq", "head"),
            P("seq", None),
            P("seq", "head"),
            P(None, "head"),
            P("head"),
            P(),
            P(),
            P("head"),
            P("head"),
            P("head"),
            P("head"),
            P("head", "seq"),
        ),
        check_vma=False,
    )
```

```python
import functools

import jax
import jax.numpy as jnp
from jax import lax
from jax.experimental import pallas as pl
from jax.experimental.pallas import tpu as pltpu
from jax.sharding import PartitionSpec as P

HEAD_DIM = 64
NST = 128
CONV = 4
CHUNK = 128
LANES = 128
EDGE = 8
GROUPS = 4
PIECES = 8

epsilon = 1e-05
f32 = jnp.float32
bf16 = jnp.bfloat16

NN = (((1,), (0,)), ((), ()))
NT = (((1,), (1,)), ((), ()))
TN = (((0,), (0,)), ((), ()))


def mm(a, b, dims=NN):
    return lax.dot_general(a, b, dims, preferred_element_type=f32)


def mm_split(a, b, dims=NN):
    high = a.astype(bf16)
    low = (a - high.astype(f32)).astype(bf16)
    return mm(high, b, dims) + mm(low, b, dims)


def mm_split_right(a, b, dims=NN):
    high = b.astype(bf16)
    rest = b - high.astype(f32)
    mid = rest.astype(bf16)
    low = (rest - mid.astype(f32)).astype(bf16)
    return mm(a, high, dims) + (mm(a, mid, dims) + mm(a, low, dims))


def sigmoid(v):
    return 1.0 / (1.0 + jnp.exp(-v))


def softplus(v):
    return jnp.maximum(v, 0.0) + jnp.log1p(jnp.exp(-jnp.abs(v)))


def iotas(rows, cols):
    return (
        lax.broadcasted_iota(jnp.int32, (rows, cols), 0),
        lax.broadcasted_iota(jnp.int32, (rows, cols), 1),
    )


def lower_ones():
    row, col = iotas(CHUNK, CHUNK)
    return (row >= col).astype(bf16)


def conv_rows(ext, taps, rows):
    total = taps[CONV : CONV + 1, :] + taps[0:1, :] * ext[EDGE - 3 : EDGE - 3 + rows, :]
    for k in range(1, CONV):
        total = total + taps[k : k + 1, :] * ext[EDGE - 3 + k : EDGE - 3 + k + rows, :]
    return total


def chunk_decays(dt_raw, heads_ref):
    step = softplus(dt_raw + heads_ref[0:1, :])
    log_decay = -jnp.exp(heads_ref[1:2, :]) * step
    cumul = mm_split_right(lower_ones(), log_decay)
    return step, cumul


def pair_weights(cumul, cumul_t, head, causal):
    differ = cumul[:, head : head + 1] - cumul_t[head : head + 1, :]
    return jnp.exp(jnp.where(causal, differ, -1e30))


def block_diag(pair, low_lanes):
    zero = jnp.zeros_like(pair)
    return jnp.concatenate(
        [jnp.where(low_lanes, pair, zero), jnp.where(low_lanes, zero, pair)], axis=0
    )


def project_kernel(
    tok_ref,
    halo_ref,
    gain_ref,
    w_ref,
    taps_ref,
    heads_ref,
    spread_ref,
    normed_ref,
    proj_ref,
    dt_ref,
    acted_ref,
    local_ref,
    cumul_ref,
    states_ref,
    total_ref,
    edge_ref,
    joined,
    state,
):
    rows = tok_ref.shape[1]
    width = spread_ref.shape[1]
    wide = width + 2 * NST
    tile = 384

    def norm(v):
        v = v.astype(f32)
        inverse = lax.rsqrt(jnp.mean(v * v, axis=-1, keepdims=True) + epsilon)
        return (v * inverse * gain_ref[...]).astype(bf16)

    edge = mm(norm(halo_ref[0]), w_ref[:, width : 2 * width + 2 * NST])
    edge = edge.astype(bf16).astype(f32)[EDGE:, :]
    joined[0:EDGE, :] = edge
    edge_ref[0] = edge
    normed_ref[0] = norm(tok_ref[0])
    for start in range(0, 2 * width, tile):
        part = mm(normed_ref[0], w_ref[:, start : start + tile]).astype(bf16)
        proj_ref[0, :, start : start + tile] = part
        if start >= width:
            joined[EDGE:, start - width : start - width + tile] = part.astype(f32)
    last = mm(normed_ref[0], w_ref[:, 2 * width :])
    part = last[:, : 2 * NST].astype(bf16)
    proj_ref[0, :, 2 * width :] = part
    joined[EDGE:, width:] = part.astype(f32)
    dt_ref[0] = last[:, 2 * NST :]

    row, col = iotas(CHUNK, CHUNK)
    causal = row >= col
    low_lanes = col < HEAD_DIM
    state[...] = jnp.zeros_like(state)

    def chunk(index, base):
        start = pl.multiple_of(index * CHUNK, CHUNK)
        here = pl.ds(start, CHUNK)
        conv = conv_rows(joined[pl.ds(start, CHUNK + EDGE), :], taps_ref, CHUNK)
        acted = conv * sigmoid(conv)
        acted_low = acted.astype(bf16)
        acted_ref[0, here, :] = acted_low
        b_low = acted_low[:, width : width + NST]
        c_low = acted_low[:, width + NST :]
        step, cumul = chunk_decays(dt_ref[0, here, :], heads_ref)
        cumul_t = cumul.T
        final = cumul[CHUNK - 1 :, :]
        cumul_ref[0, here, :] = cumul + base
        scaled = mm_split(step, spread_ref[...]) * acted[:, :width]
        scaled_low = scaled.astype(bf16)
        scores = mm(c_low, b_low, NT)
        states_ref[0, pl.ds(index, 1)] = state[...].astype(bf16)[None]
        carried = mm_split(jnp.exp(cumul), spread_ref[...]) * mm(c_low, state[...].astype(bf16))
        for pair in range(width // LANES):
            lanes = slice(pair * LANES, (pair + 1) * LANES)
            mixing = [
                (pair_weights(cumul, cumul_t, 2 * pair + k, causal) * scores).astype(bf16)
                for k in (0, 1)
            ]
            here_out = mm(
                jnp.concatenate(mixing, axis=1), block_diag(scaled_low[:, lanes], low_lanes)
            )
            local_ref[0, here, lanes] = (here_out + carried[:, lanes]).astype(bf16)
        tail = mm_split(jnp.exp(final - cumul), spread_ref[...])
        fresh = mm(b_low, (scaled * tail).astype(bf16), TN)
        keep = mm_split(jnp.broadcast_to(jnp.exp(final), (EDGE, LANES)), spread_ref[...])[0:1, :]
        state[...] = keep * state[...] + fresh
        return base + final

    base = lax.fori_loop(0, rows // CHUNK, chunk, jnp.zeros((1, LANES), f32))
    total_ref[0, 0:NST, :] = state[...].astype(bf16)
    decay = mm_split(jnp.broadcast_to(jnp.exp(base), (2 * EDGE, LANES)), spread_ref[...])
    high = decay.astype(bf16)
    first = lax.broadcasted_iota(jnp.int32, decay.shape, 0) == 0
    total_ref[0, NST:, :] = jnp.where(first, high.astype(f32), decay - high.astype(f32)).astype(bf16)


def gate_kernel(
    acted_ref,
    local_ref,
    cumul_ref,
    z_ref,
    enter_ref,
    grad_ref,
    w_out_ref,
    spread_ref,
    chan_ref,
    ssd_ref,
    gn_ref,
    sums_ref,
):
    rows = acted_ref.shape[1]
    width = spread_ref.shape[1]
    gn_ref[0] = mm(grad_ref[0], w_out_ref[...]).astype(bf16)

    def chunk(index, carry):
        here = pl.ds(pl.multiple_of(index * CHUNK, CHUNK), CHUNK)
        c_low = acted_ref[0, here, width + NST :]
        carried = mm_split(jnp.exp(cumul_ref[0, here, :]), spread_ref[...]) * mm(
            c_low, enter_ref[0]
        )
        ssd = (
            local_ref[0, here, :].astype(f32)
            + carried
            + chan_ref[1:2, :] * acted_ref[0, here, :width].astype(f32)
        )
        ssd_low = ssd.astype(bf16)
        ssd_ref[0, here, :] = ssd_low
        gate = z_ref[0, here, :].astype(f32)
        gated = ssd_low.astype(f32) * (gate * sigmoid(gate))
        square = jnp.sum(gated * gated, axis=-1, keepdims=True)
        inner = jnp.sum(
            gn_ref[0, here, :].astype(f32) * chan_ref[0:1, :] * gated, axis=-1, keepdims=True
        )
        _, col = iotas(CHUNK, LANES)
        both = jnp.where(col == 0, square, jnp.where(col == 1, inner, 0.0))
        sums_ref[0, :, here] = both.T[0:EDGE, :]
        return carry

    lax.fori_loop(0, rows // CHUNK, chunk, 0)


def mixer_kernel(
    sums_ref,
    ssd_ref,
    z_ref,
    gn_ref,
    acted_ref,
    dt_ref,
    cumul_ref,
    states_ref,
    enter_ref,
    w_out_ref,
    heads_ref,
    spread_ref,
    chan_ref,
    gnorm_ref,
    branch_ref,
    gz_ref,
    dx_ref,
    dbc_ref,
    ddt_ref,
    dld_ref,
    total_ref,
    cols_ref,
    grad_state,
    *,
    inner_total,
):
    rows = acted_ref.shape[1]
    width = spread_ref.shape[1]
    chunks = rows // CHUNK
    row, col = iotas(CHUNK, CHUNK)
    causal = row >= col
    low_lanes = col < HEAD_DIM
    grad_state[...] = jnp.zeros_like(grad_state)
    cols_ref[0] = jnp.zeros_like(cols_ref[0])
    spread = spread_ref[...]

    def chunk(turn, carry):
        index = chunks - 1 - turn
        start = pl.multiple_of(index * CHUNK, CHUNK)
        here = pl.ds(start, CHUNK)
        sums = jnp.concatenate(
            [sums_ref[0, :, here], jnp.zeros((CHUNK - EDGE, CHUNK), f32)], axis=0
        ).T
        inverse = lax.rsqrt(sums[:, 0:1] / inner_total + epsilon)
        inner_mean = inverse * sums[:, 1:2] / inner_total
        gate = z_ref[0, here, :].astype(f32)
        sig = sigmoid(gate)
        silu = gate * sig
        ssd = ssd_ref[0, here, :].astype(f32)
        unit = ssd * silu * inverse
        gnorm_ref[0, here, :] = (unit * chan_ref[0:1, :]).astype(bf16)
        gn = gn_ref[0, here, :].astype(f32)
        grad_gated = inverse * (gn * chan_ref[0:1, :] - unit * inner_mean)
        grad_ssd = grad_gated * silu
        gz_ref[0, here, :] = (grad_gated * ssd * sig * (1.0 + gate * (1.0 - sig))).astype(bf16)
        x_low = acted_ref[0, here, :width]
        x = x_low.astype(f32)
        b_low = acted_ref[0, here, width : width + NST]
        c_low = acted_ref[0, here, width + NST :]
        cols_ref[0, 0:1, :] += jnp.sum(gn * unit, axis=0, keepdims=True)
        cols_ref[0, 1:2, :] += jnp.sum(x * grad_ssd, axis=0, keepdims=True)

        step, cumul = chunk_decays(dt_ref[0, here, :], heads_ref)
        cumul_t = cumul.T
        final = cumul[CHUNK - 1 :, :]
        before = cumul_ref[0, here, :][0:1, :] - cumul[0:1, :]
        step_wide = mm_split(step, spread)
        scaled = step_wide * x
        scaled_low = scaled.astype(bf16)
        dy_low = grad_ssd.astype(bf16)
        dy = dy_low.astype(f32)
        grown = mm_split(jnp.exp(cumul), spread)
        tail = mm_split(jnp.exp(final - cumul), spread)
        keeps = mm_split(
            jnp.concatenate(
                [
                    jnp.broadcast_to(jnp.exp(final), (EDGE, LANES)),
                    jnp.broadcast_to(jnp.exp(before), (EDGE, LANES)),
                ],
                axis=0,
            ),
            spread,
        )
        keep = keeps[0:1, :]
        state = (
            states_ref[0, pl.ds(index, 1)][0].astype(f32)
            + keeps[EDGE : EDGE + 1, :] * enter_ref[0].astype(f32)
        )
        state_low = state.astype(bf16)
        later = grad_state[...]
        later_low = later.astype(bf16)
        scores = mm(c_low, b_low, NT)
        carried = grown * mm(c_low, state_low)
        tail_grad = tail * mm(b_low, later_low)
        score_grad = jnp.zeros((CHUNK, CHUNK), f32)
        rising = []
        falling = []
        for pair in range(width // LANES):
            lanes = slice(pair * LANES, (pair + 1) * LANES)
            decays = [pair_weights(cumul, cumul_t, 2 * pair + k, causal) for k in (0, 1)]
            mixing = [(d * scores).astype(bf16) for d in decays]
            scaled_two = block_diag(scaled_low[:, lanes], low_lanes)
            dy_two = block_diag(dy_low[:, lanes], low_lanes)
            out = mm(jnp.concatenate(mixing, axis=1), scaled_two)
            mixing_grad = mm(dy_low[:, lanes], scaled_two, NT)
            own_grad = mm(jnp.concatenate(mixing, axis=0), dy_two, TN)
            score_grad = (
                score_grad
                + mixing_grad[:, :CHUNK] * decays[0]
                + mixing_grad[:, CHUNK:] * decays[1]
            )
            scaled_back = scaled_low[:, lanes].astype(f32)
            rising.append(
                dy[:, lanes] * (out + carried[:, lanes]) - scaled_back * own_grad
            )
            falling.append(own_grad)
        own_all = jnp.concatenate(falling, axis=1)
        scaled_grad = own_all + tail_grad
        rise = mm_split(jnp.concatenate(rising, axis=1), spread, NT)
        fall = mm_split(scaled * tail_grad, spread, NT)
        dx_ref[0, here, :] = (step_wide * scaled_grad + chan_ref[1:2, :] * grad_ssd).astype(bf16)
        ddt_ref[0, here, :] = mm_split(x * scaled_grad, spread, NT)
        at_end = mm_split(
            jnp.broadcast_to(jnp.sum(later * state * keep, axis=0, keepdims=True), (EDGE, width)),
            spread,
            NT,
        )[0:1, :]
        upper = (row <= col).astype(bf16)
        under = (row > col).astype(bf16)
        dld_ref[0, here, :] = mm_split_right(upper, rise) + mm_split_right(under, fall) + at_end
        score_low = score_grad.astype(bf16)
        dy_grown = (dy * grown).astype(bf16)
        db = mm(score_low, c_low, TN) + mm((scaled * tail).astype(bf16), later_low, NT)
        dc = mm(score_low, b_low) + mm(dy_grown, state_low, NT)
        dbc_ref[0, here, 0:NST] = db
        dbc_ref[0, here, NST:] = dc
        grad_state[...] = keep * later + mm(c_low, dy_grown, TN)
        return carry

    lax.fori_loop(0, chunks, chunk, 0)
    total_ref[0] = grad_state[...].astype(bf16)
    branch_ref[0] = mm(gnorm_ref[0], w_out_ref[...], NT).astype(bf16)


def conv_kernel(
    proj_ref,
    edge_ref,
    acted_ref,
    dx_ref,
    dbc_ref,
    ddt_ref,
    dld_ref,
    dt_ref,
    cumul_ref,
    enter_ref,
    leave_ref,
    taps_ref,
    heads_ref,
    spread_ref,
    gj_ref,
    gdt_ref,
    first_ref,
    tapsum_ref,
    headsum_ref,
    joined,
    grads,
):
    rows = acted_ref.shape[1]
    width = spread_ref.shape[1]
    chunks = rows // CHUNK
    spread = spread_ref[...]
    joined[0:EDGE, :] = edge_ref[0]
    joined[EDGE:, :] = proj_ref[0, :, width:].astype(f32)
    tapsum_ref[0] = jnp.zeros_like(tapsum_ref[0])
    headsum_ref[0] = jnp.zeros_like(headsum_ref[0])
    grads[rows:, :] = jnp.zeros((EDGE, width + 2 * NST), f32)
    leave = leave_ref[0]
    enter = enter_ref[0]
    final = cumul_ref[0, rows - EDGE :, :][EDGE - 1 :, :]
    held = jnp.sum(leave.astype(f32) * enter.astype(f32), axis=0, keepdims=True)
    at_end = mm_split(jnp.broadcast_to(held, (EDGE, width)), spread, NT)[0:1, :] * jnp.exp(final)
    row, col = iotas(CHUNK, CHUNK)
    under = (row > col).astype(bf16)
    rate = jnp.exp(heads_ref[1:2, :])

    def chunk(index, passed):
        start = pl.multiple_of(index * CHUNK, CHUNK)
        here = pl.ds(start, CHUNK)
        conv_ext = joined[pl.ds(start, CHUNK + EDGE), :]
        conv = conv_rows(conv_ext, taps_ref, CHUNK)
        sig = sigmoid(conv)
        slope = sig * (1.0 + conv * (1.0 - sig))
        x = acted_ref[0, here, :width].astype(f32)
        b_low = acted_ref[0, here, width : width + NST]
        raw = dt_ref[0, here, :] + heads_ref[0:1, :]
        step = softplus(raw)
        step_wide = mm_split(step, spread)
        tail = mm_split(jnp.exp(final - cumul_ref[0, here, :]), spread)
        tail_grad = tail * mm(b_low, leave)
        scaled = step_wide * x
        dx = dx_ref[0, here, :].astype(f32) + step_wide * tail_grad
        db = dbc_ref[0, here, 0:NST] + mm((scaled * tail).astype(bf16), leave, NT)
        dc = dbc_ref[0, here, NST:]
        moved = mm_split(x * tail_grad, spread, NT)
        fall = moved * step
        dstep = ddt_ref[0, here, :] + moved
        dld = dld_ref[0, here, :] + mm_split_right(under, fall) + passed + at_end
        gdt = (dstep - rate * dld) * sigmoid(raw)
        gdt_ref[0, here, :] = gdt.astype(bf16)
        headsum_ref[0, 0:1, :] += jnp.sum(gdt, axis=0, keepdims=True)
        headsum_ref[0, 1:2, :] += -rate * jnp.sum(step * dld, axis=0, keepdims=True)
        grad = jnp.concatenate([dx, db, dc], axis=1) * slope
        grads[here, :] = grad
        for k in range(CONV):
            tapsum_ref[0, k : k + 1, :] += jnp.sum(
                grad * conv_ext[EDGE - 3 + k : EDGE - 3 + k + CHUNK, :], axis=0, keepdims=True
            )
        tapsum_ref[0, CONV : CONV + 1, :] += jnp.sum(grad, axis=0, keepdims=True)
        return passed + jnp.sum(fall, axis=0, keepdims=True)

    lax.fori_loop(0, chunks, chunk, jnp.zeros((1, LANES), f32))
    first_ref[0] = grads[0:EDGE, :]

    def back(index, carry):
        start = pl.multiple_of(index * CHUNK, CHUNK)
        ext = grads[pl.ds(start, CHUNK + EDGE), :]
        total = taps_ref[CONV - 1 : CONV, :] * ext[0:CHUNK, :]
        for k in range(CONV - 1):
            total = total + taps_ref[k : k + 1, :] * ext[3 - k : 3 - k + CHUNK, :]
        gj_ref[0, pl.ds(start, CHUNK), :] = total.astype(bf16)
        return carry

    lax.fori_loop(0, chunks, back, 0)


def input_kernel(gz_ref, gj_ref, gdt_ref, next_ref, taps_ref, w_ref, fixed_ref, out_ref):
    rows = gz_ref.shape[1]
    width = gz_ref.shape[2]
    wide = gj_ref.shape[2]
    ext = jnp.concatenate([jnp.zeros((2 * EDGE, wide), f32), next_ref[0]], axis=0)
    extra = jnp.zeros((2 * EDGE, wide), f32)
    for k in range(CONV - 1):
        extra = extra + taps_ref[k : k + 1, :] * ext[3 - k : 3 - k + 2 * EDGE, :]
    fixed_ref[0] = gj_ref[0]
    tail = slice(rows - 2 * EDGE, rows)
    fixed_ref[0, tail, :] = (gj_ref[0, tail, :].astype(f32) + extra).astype(bf16)
    tile = 384
    for start in range(0, out_ref.shape[2], tile):
        part = slice(start, start + tile)
        total = mm(gz_ref[0], w_ref[part, :width], NT)
        total = total + mm(fixed_ref[0], w_ref[part, width : width + wide], NT)
        total = total + mm(gdt_ref[0], w_ref[part, width + wide :], NT)
        out_ref[0, :, part] = total.astype(bf16)


def per_sequence(shape):
    zeros = (0,) * (len(shape) - 1)
    return pl.BlockSpec((1,) + tuple(shape[1:]), lambda i: (i,) + zeros)


def whole(shape):
    zeros = (0,) * len(shape)
    return pl.BlockSpec(tuple(shape), lambda i: zeros, pipeline_mode=pl.Buffered(1))


def run(body, name, count, streamed, fixed, outs, scratch, flops, order=None):
    operands = list(streamed) + list(fixed)
    moved = sum(a.size * a.dtype.itemsize for a in operands)
    moved += sum(o.size * o.dtype.itemsize for o in outs)
    return pl.pallas_call(
        body,
        name=name,
        grid=(count,),
        in_specs=[per_sequence(a.shape) for a in streamed] + [whole(a.shape) for a in fixed],
        out_specs=[per_sequence(o.shape) for o in outs],
        out_shape=outs,
        scratch_shapes=scratch,
        compiler_params=pltpu.CompilerParams(vmem_limit_bytes=60 * 1024 * 1024),
        cost_estimate=pl.CostEstimate(flops=flops, bytes_accessed=moved, transcendentals=0),
    )(*operands)


def spec(*shape, dtype=f32):
    return jax.ShapeDtypeStruct(shape, dtype)


def exchange(total, axis, forward):
    size = lax.axis_size(axis)
    place = lax.axis_index(axis)
    state = total[:, :NST].astype(f32)
    decay = jnp.sum(total[:, NST : NST + 2].astype(f32), axis=1, keepdims=True)
    met = jnp.zeros_like(state)
    met_decay = jnp.ones_like(decay)
    payload = total
    bit = 1
    while bit < size:
        got = lax.ppermute(payload, axis, [(i, i ^ bit) for i in range(size)])
        other = got[:, :NST].astype(f32)
        other_decay = jnp.sum(got[:, NST : NST + 2].astype(f32), axis=1, keepdims=True)
        upper = (place & bit) != 0
        earlier = upper if forward else jnp.logical_not(upper)
        met = jnp.where(earlier, met_decay * other + met, met)
        met_decay = jnp.where(earlier, met_decay * other_decay, met_decay)
        bit *= 2
        if bit < size:
            state = jnp.where(earlier, decay * other + state, other_decay * state + other)
            decay = decay * other_decay
            high = decay.astype(bf16)
            low = (decay - high.astype(f32)).astype(bf16)
            payload = jnp.concatenate(
                [state.astype(bf16), high, low, jnp.zeros_like(total[:, NST + 2 :])], axis=1
            )
    return met.astype(bf16)


MESH = pl.DeviceIdType.MESH


def gather_kernel(shard_ref, full_ref, own_sem, send, recv, pass_send, pass_recv):
    size = lax.axis_size("seq")
    me = lax.axis_index("seq")
    rows = shard_ref.shape[0]
    partner = me ^ 1

    def at(ref, owner):
        return ref.at[pl.ds(pl.multiple_of(owner * rows, 16), rows), :]

    def direct(k, owner, peer):
        return pltpu.make_async_remote_copy(
            src_ref=shard_ref,
            dst_ref=at(full_ref, owner),
            send_sem=send.at[k],
            recv_sem=recv.at[k],
            device_id={"seq": peer},
            device_id_type=MESH,
        )

    def passed(k, owner):
        return pltpu.make_async_remote_copy(
            src_ref=at(full_ref, owner),
            dst_ref=at(full_ref, owner),
            send_sem=pass_send.at[k],
            recv_sem=pass_recv.at[k],
            device_id={"seq": partner},
            device_id_type=MESH,
        )

    barrier = pltpu.get_barrier_semaphore()
    chips = size // 2
    for k in range(1, chips):
        pl.semaphore_signal(barrier, inc=1, device_id={"seq": me ^ (2 * k)}, device_id_type=MESH)
    pl.semaphore_signal(barrier, inc=1, device_id={"seq": partner}, device_id_type=MESH)
    pl.semaphore_wait(barrier, chips)
    for k in range(1, chips):
        direct(k, me, me ^ (2 * k)).start()
    direct(0, me, partner).start()
    own = pltpu.make_async_copy(shard_ref, at(full_ref, me), own_sem)
    own.start()
    for k in range(1, chips):
        direct(k, me ^ (2 * k), me ^ (2 * k)).wait_recv()
        passed(k, me ^ (2 * k)).start()
    direct(0, partner, partner).wait_recv()
    for k in range(1, chips):
        passed(k, partner ^ (2 * k)).wait_recv()
    for k in range(chips):
        direct(k, me, partner).wait_send()
    for k in range(1, chips):
        passed(k, me).wait_send()
    own.wait()


def gather(shard):
    size = lax.axis_size("seq")
    rows, cols = shard.shape
    chips = size // 2
    dma = pltpu.SemaphoreType.DMA
    return pl.pallas_call(
        gather_kernel,
        name="gather",
        in_specs=[pl.BlockSpec(memory_space=pltpu.VMEM)],
        out_specs=pl.BlockSpec(memory_space=pl.ANY),
        out_shape=jax.ShapeDtypeStruct((size * rows, cols), shard.dtype),
        scratch_shapes=[dma, dma((chips,)), dma((chips,)), dma((chips,)), dma((chips,))],
        compiler_params=pltpu.CompilerParams(collective_id=0, has_side_effects=True),
        cost_estimate=pl.CostEstimate(
            flops=0, bytes_accessed=40 * size * rows * cols, transcendentals=0
        ),
    )(shard)


def tail_kernel(
    part_ref,
    tok_ref,
    og_ref,
    gain_ref,
    wg_ref,
    vg_ref,
    small_ref,
    tg_ref,
    ws_ref,
    vs_ref,
    bc_ref,
    smallsum_ref,
    tapsum_ref,
    gainsum_ref,
    recv,
    result,
    wrecv,
    vrecv,
    srecv,
    grecv,
    gown,
    zown,
    zrecv,
    town,
    trecv,
    rs_send,
    rs_recv,
    ag_send,
    ag_recv,
    peer_send,
    peer_recv,
    own_sem,
    z_send,
    z_recv,
    *,
    width,
):
    pieces, size = part_ref.shape[0], part_ref.shape[1]
    node = lax.axis_index("head")
    peers = lax.axis_size("seq")
    me = lax.axis_index("seq")
    shard = ws_ref.shape[0]
    last = size - 1
    right, left = node + 1, node - 1

    barrier = pltpu.get_barrier_semaphore()
    for k in range(1, peers):
        pl.semaphore_signal(barrier, inc=1, device_id={"seq": me ^ k}, device_id_type=MESH)
    for k in range(1, size):
        pl.semaphore_signal(
            barrier, inc=1, device_id={"head": lax.rem(node + k, size)}, device_id_type=MESH
        )
    pl.semaphore_wait(barrier, peers + size - 2)

    def slab(ref, owner):
        return ref.at[pl.ds(pl.multiple_of(owner * shard, 16), shard), :]

    def peer_copies(k, dest, slot):
        def one(index, src, dst):
            return pltpu.make_async_remote_copy(
                src_ref=src,
                dst_ref=dst,
                send_sem=peer_send.at[index, k],
                recv_sem=peer_recv.at[index, k],
                device_id={"seq": dest},
                device_id_type=MESH,
            )

        return (
            one(0, slab(wg_ref, dest), wrecv.at[slot]),
            one(1, slab(vg_ref, dest), vrecv.at[slot]),
            one(2, small_ref, srecv.at[slot]),
        )

    def gain_copy(k, dest, slot):
        return pltpu.make_async_remote_copy(
            src_ref=gown,
            dst_ref=grecv.at[slot],
            send_sem=peer_send.at[3, k],
            recv_sem=peer_recv.at[3, k],
            device_id={"seq": dest},
            device_id_type=MESH,
        )

    def z_copies(k, dest, slot):
        def one(index, src, dst):
            return pltpu.make_async_remote_copy(
                src_ref=src,
                dst_ref=dst,
                send_sem=z_send.at[index, k],
                recv_sem=z_recv.at[index, k],
                device_id={"head": dest},
                device_id_type=MESH,
            )

        return (one(0, zown, zrecv.at[slot]), one(1, town, trecv.at[slot]))

    for k in range(1, peers):
        for copy in peer_copies(k, me ^ k, k):
            copy.start()
    own_w = pltpu.make_async_copy(slab(wg_ref, me), wrecv.at[0], own_sem.at[0])
    own_v = pltpu.make_async_copy(slab(vg_ref, me), vrecv.at[0], own_sem.at[1])
    own_w.start()
    own_v.start()
    gown[...] = jnp.zeros_like(gown)

    def rs_copy(k, chunk, src, slot, dest):
        return pltpu.make_async_remote_copy(
            src_ref=src,
            dst_ref=recv.at[k, slot],
            send_sem=rs_send.at[k, chunk],
            recv_sem=rs_recv.at[k, slot],
            device_id={"head": dest},
            device_id_type=MESH,
        )

    def ag_copy(k, chunk, sem, dest):
        return pltpu.make_async_remote_copy(
            src_ref=result.at[k, chunk],
            dst_ref=result.at[k, chunk],
            send_sem=ag_send.at[k, sem],
            recv_sem=ag_recv.at[k, chunk],
            device_id={"head": dest},
            device_id_type=MESH,
        )

    def arrived(k, slot):
        rs_copy(k, 0, recv.at[k, slot], slot, node).wait_recv()

    def add_own(k, chunk):
        recv[k, chunk] = (recv[k, chunk].astype(f32) + part_ref[k, chunk].astype(f32)).astype(bf16)

    def reduce_step(k, step):
        @pl.when((node <= step) & (node < last))
        def _():
            chunk = last - step + node

            @pl.when(node > 0)
            def _():
                arrived(k, chunk)
                add_own(k, chunk)
                rs_copy(k, chunk, recv.at[k, chunk], chunk, right).start()

            @pl.when(node == 0)
            def _():
                rs_copy(k, chunk, part_ref.at[k, chunk], chunk, right).start()

        @pl.when((last - node <= step) & (node > 0))
        def _():
            chunk = step - (last - node)
            slot = jnp.where(chunk == node - 1, size, chunk)

            @pl.when(node < last)
            def _():
                arrived(k, chunk)
                add_own(k, chunk)
                rs_copy(k, chunk, recv.at[k, chunk], slot, left).start()

            @pl.when(node == last)
            def _():
                rs_copy(k, chunk, part_ref.at[k, chunk], slot, left).start()

    def emit(k, chunk):
        hidden = tok_ref[k, chunk].astype(f32)
        inverse = lax.rsqrt(jnp.mean(hidden * hidden, axis=-1, keepdims=True) + epsilon)
        unit = hidden * inverse
        grad = result[k, chunk].astype(f32)
        both = grad * unit
        gown[0:1, :] += jnp.sum(both, axis=0, keepdims=True)
        inner = jnp.mean(both * gain_ref[...], axis=-1, keepdims=True)
        tg_ref[k, chunk] = (
            og_ref[k, chunk].astype(f32) + inverse * (grad * gain_ref[...] - unit * inner)
        ).astype(bf16)

    def own_step(k):
        @pl.when(node > 0)
        def _():
            arrived(k, node)

        @pl.when(node < last)
        def _():
            arrived(k, size)

        total = part_ref[k, node].astype(f32)
        zero = jnp.zeros_like(total)
        total = total + jnp.where(node > 0, recv[k, node].astype(f32), zero)
        total = total + jnp.where(node < last, recv[k, size].astype(f32), zero)
        result[k, node] = total.astype(bf16)

        @pl.when(node < last)
        def _():
            ag_copy(k, node, node, right).start()

        @pl.when(node > 0)
        def _():
            ag_copy(k, node, size, left).start()

        emit(k, node)

    def pass_step(k, away):
        @pl.when(node - away >= 0)
        def _():
            chunk = node - away
            ag_copy(k, chunk, chunk, node).wait_recv()

            @pl.when(node < last)
            def _():
                ag_copy(k, chunk, chunk, right).start()

            emit(k, chunk)

        @pl.when(node + away <= last)
        def _():
            chunk = node + away
            ag_copy(k, chunk, chunk, node).wait_recv()

            @pl.when(node > 0)
            def _():
                ag_copy(k, chunk, chunk, left).start()

            emit(k, chunk)

    def finish_weights():
        for k in range(1, peers):
            for copy in peer_copies(k, me ^ k, k):
                copy.wait_recv()
        own_w.wait()
        own_v.wait()

        def rows(step, carry):
            here = pl.ds(pl.multiple_of(step * 16, 16), 16)
            total = wrecv[0, here, :].astype(f32)
            other = vrecv[0, here, :].astype(f32)
            for k in range(1, peers):
                total = total + wrecv[k, here, :].astype(f32)
                other = other + vrecv[k, here, :].astype(f32)
            ws_ref[here, :] = total
            vs_ref[here, :] = other
            zown[here, :] = total[:, 2 * width : 2 * width + 2 * NST].astype(bf16)
            return carry

        lax.fori_loop(0, shard // 16, rows, 0)
        total = small_ref[...]
        for k in range(1, peers):
            total = total + srecv[k]
        smallsum_ref[...] = total
        town[...] = total[0:EDGE, width:]
        for k in range(1, size):
            for copy in z_copies(k, lax.rem(node + k, size), k):
                copy.start()

    steps = 2 * last

    def tick(t, carry):
        for s in range(steps + 1):
            k = t - s

            @pl.when((k >= 0) & (k < pieces))
            def _():
                if s < last:
                    reduce_step(k, s)
                elif s == last:
                    own_step(k)
                else:
                    pass_step(k, s - last)

        @pl.when(t == pieces)
        def _():
            finish_weights()

        return carry

    lax.fori_loop(0, pieces + steps, tick, 0)

    for k in range(1, peers):
        gain_copy(k, me ^ k, k).start()
    for k in range(1, size):
        for copy in z_copies(k, node, k):
            copy.wait_recv()
    total = zown[...].astype(f32)
    taps = town[...]
    for k in range(1, size):
        total = total + zrecv[k].astype(f32)
        taps = taps + trecv[k]
    bc_ref[...] = total
    tapsum_ref[...] = taps
    for k in range(1, peers):
        gain_copy(k, me ^ k, k).wait_recv()
    gain = gown[...]
    for k in range(1, peers):
        gain = gain + grecv[k]
    gainsum_ref[...] = gain

    def drain(k, carry):
        for chunk in range(size):

            @pl.when(chunk != node)
            def _():
                rs_copy(k, chunk, recv.at[k, chunk], chunk, node).wait_send()

            @pl.when((chunk < node) & (node < last) | (chunk > node) & (node > 0))
            def _():
                ag_copy(k, chunk, chunk, node).wait_send()

        @pl.when(node < last)
        def _():
            ag_copy(k, node, node, node).wait_send()

        @pl.when(node > 0)
        def _():
            ag_copy(k, node, size, node).wait_send()

        return carry

    lax.fori_loop(0, pieces, drain, 0)
    for k in range(1, peers):
        for copy in peer_copies(k, me ^ k, k):
            copy.wait_send()
        gain_copy(k, me ^ k, k).wait_send()
    for k in range(1, size):
        for copy in z_copies(k, node, k):
            copy.wait_send()


def tail(part, tokens, grads, gain, wg, vg, small, width):
    pieces, size, rows, model = part.shape
    peers = lax.axis_size("seq")
    shard = wg.shape[0] // peers
    cols, wide = wg.shape[1], small.shape[1]
    dma = pltpu.SemaphoreType.DMA
    vmem = pl.BlockSpec(memory_space=pltpu.VMEM)
    hbm = pl.BlockSpec(memory_space=pl.ANY)
    return pl.pallas_call(
        functools.partial(tail_kernel, width=width),
        name="tail",
        in_specs=[vmem, vmem, vmem, vmem, hbm, hbm, vmem],
        out_specs=[vmem] * 7,
        out_shape=[
            spec(pieces, size, rows, model, dtype=bf16),
            spec(shard, cols),
            spec(shard, width),
            spec(shard, 2 * NST),
            spec(*small.shape),
            spec(EDGE, 2 * NST),
            spec(EDGE, model),
        ],
        scratch_shapes=[
            pltpu.VMEM((pieces, size + 1, rows, model), bf16),
            pltpu.VMEM((pieces, size, rows, model), bf16),
            pltpu.VMEM((peers, shard, cols), bf16),
            pltpu.VMEM((peers, shard, width), bf16),
            pltpu.VMEM((peers,) + small.shape, f32),
            pltpu.VMEM((peers, EDGE, model), f32),
            pltpu.VMEM((EDGE, model), f32),
            pltpu.VMEM((shard, 2 * NST), bf16),
            pltpu.VMEM((size, shard, 2 * NST), bf16),
            pltpu.VMEM((EDGE, 2 * NST), f32),
            pltpu.VMEM((size, EDGE, 2 * NST), f32),
            dma((pieces, size)),
            dma((pieces, size + 1)),
            dma((pieces, size + 1)),
            dma((pieces, size)),
            dma((4, peers)),
            dma((4, peers)),
            dma((2,)),
            dma((2, size)),
            dma((2, size)),
        ],
        compiler_params=pltpu.CompilerParams(
            collective_id=1, has_side_effects=True, vmem_limit_bytes=63 * 1024 * 1024
        ),
        cost_estimate=pl.CostEstimate(
            flops=0, bytes_accessed=60 * part.size, transcendentals=0
        ),
    )(part, tokens, grads, gain, wg, vg, small)


def sum_over_heads(value):
    size = lax.axis_size("head")
    total = value
    for k in range(1, size):
        total = total + lax.ppermute(value, "head", [(i, (i + k) % size) for i in range(size)])
    return total


def local(
    tokens,
    norm_gain,
    w_z,
    w_x,
    w_bc,
    w_dt,
    conv_x,
    conv_x_bias,
    conv_bc,
    conv_bc_bias,
    dt_bias,
    a_log,
    d_skip,
    gate_gain,
    w_out,
    lengths,
    out_grad,
):
    micro, seqs, rows, model = tokens.shape
    batch = micro * seqs
    width = w_z.shape[1]
    heads = width // HEAD_DIM
    wide = width + 2 * NST
    inner_total = width * lax.axis_size("head")
    per = batch // GROUPS
    flat = tokens.reshape(batch, rows, model)
    flat_grad = out_grad.reshape(batch, rows, model)

    seq_size = lax.axis_size("seq")
    halo = lax.ppermute(
        flat[:, rows - 2 * EDGE :, :], "seq", [(i, i + 1) for i in range(seq_size - 1)]
    )
    keep_rows = jnp.arange(2 * EDGE) >= 2 * EDGE - (CONV - 1)
    halo = jnp.where(keep_rows[None, :, None], halo, jnp.zeros_like(halo))

    w_shard = jnp.concatenate(
        [w_z, w_x, w_bc, w_dt, jnp.zeros((w_dt.shape[0], LANES - heads), bf16)], axis=1
    )
    w_all = gather(w_shard)
    w_back = lax.all_gather(w_out.T, "seq", axis=0, tiled=True)

    positions = lax.axis_index("seq") * rows + jnp.arange(rows, dtype=jnp.int32)
    valid = positions[None, :] < lengths.reshape(batch)[:, None]
    grad_branch = jnp.where(valid[:, :, None], flat_grad, jnp.zeros_like(flat_grad))

    taps = jnp.concatenate(
        [
            jnp.concatenate([conv_x, conv_bc], axis=1),
            jnp.concatenate([conv_x_bias, conv_bc_bias])[None],
            jnp.zeros((EDGE - CONV - 1, wide), f32),
        ],
        axis=0,
    )
    pad = LANES - heads
    head_rows = jnp.concatenate(
        [
            jnp.concatenate([dt_bias, jnp.full((pad,), -1e4, f32)])[None],
            jnp.concatenate([a_log, jnp.zeros((pad,), f32)])[None],
            jnp.zeros((EDGE - 2, LANES), f32),
        ],
        axis=0,
    )
    spread = (
        jnp.arange(LANES)[:, None] == (jnp.arange(width) // HEAD_DIM)[None, :]
    ).astype(bf16)
    chan = jnp.concatenate(
        [
            gate_gain[None],
            jnp.repeat(d_skip, HEAD_DIM)[None],
            jnp.zeros((EDGE - 2, width), f32),
        ],
        axis=0,
    )
    chunks = rows // CHUNK

    first = []
    for g in range(GROUPS):
        part = slice(g * per, (g + 1) * per)
        first.append(
            run(
                project_kernel,
                "project",
                per,
                [flat[part], halo[part]],
                [norm_gain[None], w_all, taps, head_rows, spread],
                [
                    spec(per, rows, model, dtype=bf16),
                    spec(per, rows, 2 * width + 2 * NST, dtype=bf16),
                    spec(per, rows, LANES),
                    spec(per, rows, wide, dtype=bf16),
                    spec(per, rows, width, dtype=bf16),
                    spec(per, rows, LANES),
                    spec(per, chunks, NST, width, dtype=bf16),
                    spec(per, NST + 2 * EDGE, width, dtype=bf16),
                    spec(per, EDGE, wide),
                ],
                [pltpu.VMEM((rows + EDGE, wide), f32), pltpu.VMEM((NST, width), f32)],
                2 * per * rows * model * w_all.shape[1],
            )
        )
    entering = [exchange(first[g][7], "seq", True) for g in range(GROUPS)]

    second = []
    for g in range(GROUPS):
        part = slice(g * per, (g + 1) * per)
        _, proj, _, acted, own, cumul, _, _, _ = first[g]
        second.append(
            run(
                gate_kernel,
                "gate",
                per,
                [acted, own, cumul, proj[:, :, :width], entering[g], grad_branch[part]],
                [w_back, spread, chan],
                [
                    spec(per, rows, width, dtype=bf16),
                    spec(per, rows, width, dtype=bf16),
                    spec(per, EDGE, rows),
                ],
                [],
                2 * per * rows * model * width,
            )
        )
    sums = [sum_over_heads(second[g][2]) for g in range(GROUPS)]

    third = []
    for g in range(GROUPS):
        _, proj, dt_raw, acted, _, cumul, states, _, _ = first[g]
        ssd, gn, _ = second[g]
        third.append(
            run(
                functools.partial(mixer_kernel, inner_total=inner_total),
                "mixer",
                per,
                [
                    sums[g],
                    ssd,
                    proj[:, :, :width],
                    gn,
                    acted,
                    dt_raw,
                    cumul,
                    states,
                    entering[g],
                ],
                [w_back, head_rows, spread, chan],
                [
                    spec(per, rows, width, dtype=bf16),
                    spec(per, rows, model, dtype=bf16),
                    spec(per, rows, width, dtype=bf16),
                    spec(per, rows, width, dtype=bf16),
                    spec(per, rows, 2 * NST),
                    spec(per, rows, LANES),
                    spec(per, rows, LANES),
                    spec(per, NST, width, dtype=bf16),
                    spec(per, EDGE, width),
                ],
                [pltpu.VMEM((NST, width), f32)],
                2 * per * rows * model * width,
            )
        )
    branches = [lax.psum(third[g][1], "head") for g in range(GROUPS)]
    leaving = [
        exchange(
            jnp.concatenate([third[g][7], first[g][7][:, NST:]], axis=1), "seq", False
        )
        for g in range(GROUPS)
    ]

    fourth = []
    for g in range(GROUPS):
        _, proj, dt_raw, acted, _, cumul, _, _, edge = first[g]
        _, _, _, dx, dbc, ddt, dld, _, _ = third[g]
        fourth.append(
            run(
                conv_kernel,
                "conv",
                per,
                [proj, edge, acted, dx, dbc, ddt, dld, dt_raw, cumul, entering[g], leaving[g]],
                [taps, head_rows, spread],
                [
                    spec(per, rows, wide, dtype=bf16),
                    spec(per, rows, LANES, dtype=bf16),
                    spec(per, EDGE, wide),
                    spec(per, EDGE, wide),
                    spec(per, EDGE, LANES),
                ],
                [pltpu.VMEM((rows + EDGE, wide), f32), pltpu.VMEM((rows + EDGE, wide), f32)],
                per * rows * wide * 60,
            )
        )
    nexts = [
        lax.ppermute(fourth[g][2], "seq", [(i + 1, i) for i in range(seq_size - 1)])
        for g in range(GROUPS)
    ]

    fifth = []
    for g in range(GROUPS):
        gj, gdt, _, _, _ = fourth[g]
        fifth.append(
            run(
                input_kernel,
                "input_grad",
                per,
                [third[g][2], gj, gdt, nexts[g]],
                [taps, w_all],
                [spec(per, rows, wide, dtype=bf16), spec(per, rows, model, dtype=bf16)],
                [],
                2 * per * rows * model * w_all.shape[1],
            )
        )

    def joined(parts):
        return jnp.concatenate(parts, axis=0).reshape(batch * rows, -1)

    normed = joined([f[0] for f in first])
    gz = joined([t[2] for t in third])
    gj = joined([t[0] for t in fifth])
    gdt = joined([t[1] for t in fourth])
    gnorm = joined([t[0] for t in third])
    w_grad = jnp.concatenate(
        [mm(normed, gz, TN), mm(normed, gj, TN), mm(normed, gdt, TN)], axis=1
    ).astype(bf16)
    out_w_grad = mm(grad_branch.reshape(batch * rows, model), gnorm, TN).astype(bf16)

    cols = sum(jnp.sum(t[8], axis=0) for t in third)
    tap_sum = sum(jnp.sum(t[3], axis=0) for t in fourth)
    head_sum = sum(jnp.sum(t[4], axis=0) for t in fourth)
    small = jnp.concatenate(
        [
            tap_sum,
            jnp.concatenate([cols, jnp.zeros((EDGE, wide - width), f32)], axis=1),
            jnp.concatenate([head_sum, jnp.zeros((EDGE, wide - LANES), f32)], axis=1),
        ],
        axis=0,
    )
    head_size = lax.axis_size("head")
    cut = (PIECES, head_size, batch * rows // (PIECES * head_size), model)
    partial_in = jnp.concatenate([t[1] for t in fifth], axis=0)
    input_grads, w_sum, out_w_sum, bc_sum, small, bc_taps, gain_grad = tail(
        partial_in.reshape(cut),
        flat.reshape(cut),
        flat_grad.reshape(cut),
        norm_gain[None],
        w_grad,
        out_w_grad,
        small,
        width,
    )
    skip = jnp.sum(small[EDGE + 1, :width].reshape(heads, HEAD_DIM), axis=1)

    layer_outs = []
    for g in range(GROUPS):
        part = slice(g * per, (g + 1) * per)
        hidden = flat[part].astype(f32)
        layer_outs.append(
            jnp.where(
                valid[part][:, :, None], hidden + branches[g].astype(f32), hidden
            ).astype(bf16)
        )

    out_shape = (micro, seqs, rows, model)
    return (
        jnp.concatenate(layer_outs, axis=0).reshape(out_shape),
        input_grads.reshape(out_shape),
        gain_grad[0],
        w_sum[:, :width],
        w_sum[:, width : 2 * width],
        bc_sum,
        w_sum[:, 2 * width + 2 * NST : 2 * width + 2 * NST + heads],
        small[:CONV, :width],
        small[CONV, :width],
        bc_taps[:CONV],
        bc_taps[CONV],
        small[2 * EDGE, :heads],
        small[2 * EDGE + 1, :heads],
        skip,
        small[EDGE, :width],
        out_w_sum.T,
    )


def solution(mesh):
    placed = (
        P(None, None, "seq", None),
        P(),
        P("seq", "head"),
        P("seq", "head"),
        P("seq", None),
        P("seq", "head"),
        P(None, "head"),
        P("head"),
        P(),
        P(),
        P("head"),
        P("head"),
        P("head"),
        P("head"),
        P("head", "seq"),
        P(),
        P(None, None, "seq", None),
    )
    return jax.shard_map(
        local,
        mesh=mesh,
        in_specs=placed,
        out_specs=(
            P(None, None, "seq", None),
            P(None, None, "seq", None),
            P(),
            P("seq", "head"),
            P("seq", "head"),
            P("seq", None),
            P("seq", "head"),
            P(None, "head"),
            P("head"),
            P(),
            P(),
            P("head"),
            P("head"),
            P("head"),
            P("head"),
            P("head", "seq"),
        ),
        check_vma=False,
    )
```
